768 devices in a mesh: segment: 12 (over z_lo, core), ctx: 8 (over z_hi, x), head: 8 (over y).
Axes of the slice: x: 4, y: 8, z: 12 (z_hi: 2, z_lo: 6; z = z_hi * 6 + z_lo), core: 2. Of those that a mesh axis runs over, the one named last changes fastest.
Arguments:
- queries: bfloat16 [1536, 8192], P('segment', 'head'), may hold values from -6 to 6
- keys: bfloat16 [196608, 1024], P(('segment', 'ctx'), 'head'), may hold values from -6 to 6
- values: bfloat16 [196608, 1024], P(('segment', 'ctx'), 'head'), may hold values from -6 to 6
- lengths: int32 [12], P('segment'), may hold values from 6145 to 16384, as said below
- selected: int32 [12, 3], P('segment'), may hold values from 0 to 7, as said below
- out_weight: bfloat16 [8192, 8192], P(('head', 'ctx')), may hold values from -3 to 3
Outputs:
- handed: bfloat16 [1536, 8192], P('segment', ('head', 'ctx'))
The draws below stay inside these ranges and needn't reach their ends.
Inputs may be any that keep to these rules, and one draw needn't show every extreme that they name: `lengths`: Even-indexed sections hold 8192 cached positions or fewer, odd-indexed ones more than 8192; some section holds exactly 16384. `selected`: each row names 3 distinct blocks, each holding at least one cached position of its section; block 0 and the block holding the section's last cached position are always named.
All inputs are finite; a program needn't handle non-finite values.
Results may differ from the reference program's by a relative error of at most 0.019.
Values may be sent and summed in bfloat16 or wider, within the bound.
No kernel may reach another device: no remote copies, remote signals or barrier semaphores. Data moves between devices by JAX's collectives and lax.ppermute only.
A program may use at most 32 MiB of HBM per device.

```python
import math
import jax
import jax.numpy as jnp
from jax import lax

D = 8192
QUERY_HEADS = 64
KV_HEADS_COUNT = 8
HEAD_DIM = 128
SLICE_ROWS = 128
BLOCK = 2048
SEL = 3
LIGHT = 8192
SECTION_CACHE = 16384
QROWS = 1536
ALL_CACHE_ROWS = 196608
N_SEGMENT = 12


def lengths_and_blocks(key):
    base = jax.random.fold_in(key, 11)
    key_light, key_heavy, key_full, key_rank = jax.random.split(base, 4)
    section_count = QROWS // SLICE_ROWS
    segment_ids = jnp.arange(section_count, dtype=jnp.int32)
    light = jax.random.randint(key_light, (section_count,), SEL * BLOCK + 1, LIGHT + 1)
    heavy = jax.random.randint(key_heavy, (section_count,), LIGHT + 1, SECTION_CACHE + 1)
    full_at = 2 * jax.random.randint(key_full, (), 0, section_count // 2) + 1
    cached = jnp.where(segment_ids % 2 == 1, heavy, light)
    cached = jnp.where(segment_ids == full_at, SECTION_CACHE, cached).astype(jnp.int32)
    block_count = SECTION_CACHE // BLOCK
    last_block = (cached - 1) // BLOCK
    ranks = jax.vmap(lambda sub: jax.random.permutation(sub, block_count))(jax.random.split(key_rank, section_count))
    block_ids = jnp.arange(block_count, dtype=jnp.int32)[None, :]
    inside = (block_ids >= 1) & (block_ids < last_block[:, None])
    score = jnp.where(inside, ranks.astype(jnp.int32), block_count + block_ids)
    order = jnp.argsort(score, axis=1, stable=True)[:, :SEL - 2].astype(jnp.int32)
    chosen = jnp.concatenate([jnp.zeros((section_count, 1), jnp.int32), order, last_block[:, None].astype(jnp.int32)], axis=1)
    return (cached, chosen.astype(jnp.int32))


def draw_lengths(key, part):
    return lengths_and_blocks(key)[0]


def draw_selected(key, part):
    return lengths_and_blocks(key)[1]


def draw_queries(key, part):
    inner_function = jax.random.fold_in(key, 31)
    sampled_blocks = jnp.clip(jax.random.normal(inner_function, (QROWS, QUERY_HEADS * HEAD_DIM), jnp.float32), -5.0, 5.0)
    return sampled_blocks.astype(jnp.bfloat16)


def draw_keys(key, part):
    inner_function = jax.random.fold_in(key, 37)
    sampled_blocks = jnp.clip(jax.random.normal(inner_function, (ALL_CACHE_ROWS, KV_HEADS_COUNT * HEAD_DIM), jnp.float32), -5.0, 5.0)
    return sampled_blocks.astype(jnp.bfloat16)


def block_levels(stream_key, shape, cuts, least, largest):
    def one(dim, parts):
        steps = jax.random.uniform(jax.random.fold_in(jax.random.fold_in(stream_key, 6), dim), (parts,), jnp.float32, least / len(cuts), largest / len(cuts))
        return jnp.repeat(jnp.exp(steps), shape[dim] // parts).reshape((-1,) + (1,) * (len(shape) - dim - 1))

    level = one(*cuts[0])
    for cut in cuts[1:]:
        level = level * one(*cut)
    return level


def centred(key, extent, deviation, bound, pieces=(), held_as=jnp.bfloat16):
    values = jax.random.normal(key, extent, jnp.float32) * deviation
    if len(pieces) > 0:
        values = block_levels(key, extent, pieces, -0.22, 0.18) * values
    return jnp.clip(values, min=-bound, max=bound).astype(held_as)


def setup_inputs(seed: int = 0) -> dict:
    splits = jax.random.split(jax.random.key(seed), 7)
    queries = draw_queries(jax.random.fold_in(splits[6], 71), 0)
    keys = draw_keys(jax.random.fold_in(splits[6], 71), 0)
    values = centred(splits[2], (ALL_CACHE_ROWS, KV_HEADS_COUNT * HEAD_DIM), 1.0, 6.0, ((0, 96), (1, 8)))
    lengths = draw_lengths(jax.random.fold_in(splits[6], 71), 0)
    selected = draw_selected(jax.random.fold_in(splits[6], 71), 0)
    out_weight = centred(splits[5], (QUERY_HEADS * HEAD_DIM, D), 0.5, 3.0, ((0, 64),))
    return {"queries": queries, "keys": keys, "values": values, "lengths": lengths, "selected": selected, "out_weight": out_weight}


MASKED = -1e+30

def reference(queries, keys, values, lengths, selected, out_weight):
    heads_per_group = QUERY_HEADS // KV_HEADS_COUNT
    score_scale = 1.0 / math.sqrt(HEAD_DIM)
    every_query = queries.reshape(N_SEGMENT, SLICE_ROWS, KV_HEADS_COUNT, heads_per_group, HEAD_DIM)
    every_key = keys.reshape(N_SEGMENT, SECTION_CACHE, KV_HEADS_COUNT, HEAD_DIM)
    every_value = values.reshape(N_SEGMENT, SECTION_CACHE, KV_HEADS_COUNT, HEAD_DIM)

    def one_segment(segment_args):
        query_part, key_part, value_part, length, chosen = segment_args
        positions = (chosen[:, None] * BLOCK + jnp.arange(BLOCK, dtype=jnp.int32)[None, :]).reshape(-1).astype(jnp.int32)
        usable = positions < length
        key_sel = key_part[positions]
        value_sel = value_part[positions]

        def one_head(head_args):
            query_head, key_head, value_head = head_args
            scores = jnp.einsum('rgd,pd->rgp', query_head.astype(jnp.float32), key_head.astype(jnp.float32)) * score_scale
            scores = jnp.where(usable[None, None, :], scores, MASKED)
            top = lax.optimization_barrier(jnp.max(scores, axis=-1, keepdims=True))
            expo = jnp.where(usable[None, None, :], jnp.exp(scores - top), 0.0)
            total = lax.optimization_barrier(jnp.sum(expo, axis=-1))
            weights = lax.optimization_barrier(expo.astype(jnp.bfloat16))
            summed = jnp.einsum('rgp,pd->rgd', weights.astype(jnp.float32), value_head.astype(jnp.float32))
            return (summed / total[..., None]).astype(jnp.bfloat16)
        heads_out = lax.map(one_head, (query_part.transpose(1, 0, 2, 3), key_sel.transpose(1, 0, 2), value_sel.transpose(1, 0, 2)))
        attention = heads_out.transpose(1, 0, 2, 3).reshape(SLICE_ROWS, QUERY_HEADS * HEAD_DIM)
        return jnp.dot(attention, out_weight, preferred_element_type=jnp.float32)
    projected = lax.map(one_segment, (every_query, every_key, every_value, lengths, selected))
    handed = jnp.roll(projected, 1, axis=0).astype(jnp.bfloat16)
    return handed.reshape(N_SEGMENT * SLICE_ROWS, D)
```

```python
import functools
import math

import jax
import jax.numpy as jnp
from jax import lax
from jax.experimental import pallas as pl
from jax.experimental.pallas import tpu as pltpu
from jax.sharding import PartitionSpec as P

HEAD_DIM = 128
BLOCK = 2048
STAT_ROWS = 16
MASKED = -1e30
LOG2E = 1.4426950408889634
Z_PARTS = 2


def whole(count):
    return [pl.BlockSpec(memory_space=pltpu.VMEM)] * count


def stat_rows(lse):
    high = lse.astype(jnp.bfloat16).astype(jnp.float32)
    rest = lse - high
    mid = rest.astype(jnp.bfloat16).astype(jnp.float32)
    low = rest - mid
    row = lax.broadcasted_iota(jnp.int32, (STAT_ROWS, lse.shape[1]), 0)
    return jnp.where(row == 0, high, jnp.where(row == 1, mid, low)).astype(jnp.bfloat16)


def attend_body(cached_ref, chosen_ref, q_ref, k_ref, v_ref, out_ref, vt_ref, *, together):
    x_parts, z_parts = out_ref.shape[:2]
    rows = q_ref.shape[0]
    span = k_ref.shape[0]
    block_id = lax.axis_index("z") * x_parts + lax.axis_index("x")
    usable = cached_ref[0] - block_id * span
    picked = usable > 0
    named = chosen_ref[0, 0] == block_id
    for i in range(1, chosen_ref.shape[1]):
        named = jnp.logical_or(named, chosen_ref[0, i] == block_id)
    picked = jnp.logical_and(picked, named)
    factor = LOG2E / math.sqrt(HEAD_DIM)

    @pl.when(jnp.logical_not(picked))
    def _():
        for x in range(x_parts):
            for z in range(z_parts):
                out_ref[x, z, :HEAD_DIM, :] = jnp.zeros((HEAD_DIM, rows), jnp.bfloat16)
                out_ref[x, z, HEAD_DIM:, :] = jnp.full((STAT_ROWS, rows), MASKED, jnp.bfloat16)

    @pl.when(picked)
    def _():
        vt_ref[...] = v_ref[...].T
        position = lax.broadcasted_iota(jnp.int32, (span, 1), 0)
        for first in range(0, x_parts * z_parts, together):
            heads = [q_ref[:, (first + i) * HEAD_DIM : (first + i + 1) * HEAD_DIM] for i in range(together)]
            scores = lax.dot_general(
                k_ref[...],
                jnp.concatenate(heads, axis=0),
                (((1,), (1,)), ((), ())),
                preferred_element_type=jnp.float32,
            )
            scores = jnp.where(position < usable, scores, MASKED)
            top = jnp.max(scores, axis=0, keepdims=True)
            expo = jnp.exp2((scores - top) * factor)
            total = jnp.sum(expo, axis=0, keepdims=True)
            gathered = jnp.dot(vt_ref[...], expo.astype(jnp.bfloat16), preferred_element_type=jnp.float32)
            gathered = (gathered / total).astype(jnp.bfloat16)
            stats = stat_rows(top * factor + jnp.log2(total))
            for i in range(together):
                z, x = divmod(first + i, x_parts)
                out_ref[x, z, :HEAD_DIM, :] = gathered[:, i * rows : (i + 1) * rows]
                out_ref[x, z, HEAD_DIM:, :] = stats[:, i * rows : (i + 1) * rows]


def merged(parts):
    logs = []
    for part in parts:
        stats = part[HEAD_DIM:, :].astype(jnp.float32)
        logs.append(stats[0:1] + stats[1:2] + stats[2:3])
    top = functools.reduce(jnp.maximum, logs)
    shares = [jnp.exp2(log - top) for log in logs]
    total = functools.reduce(jnp.add, shares)
    summed = functools.reduce(
        jnp.add, [part[:HEAD_DIM, :].astype(jnp.float32) * (share / total) for part, share in zip(parts, shares)]
    )
    return summed, top + jnp.log2(total)


def merge_body(parts_ref, own_ref, cross_ref):
    z = lax.axis_index("z")
    for ref, head in ((cross_ref, 1 - z), (own_ref, z)):
        out, log = merged([parts_ref[i, head] for i in range(parts_ref.shape[0])])
        ref[:HEAD_DIM, :] = out.astype(jnp.bfloat16)
        ref[HEAD_DIM:, :] = stat_rows(log)


def project_body(own_ref, other_ref, weight_ref, out_ref):
    out, _ = merged([own_ref[...], other_ref[...]])
    rows = out.T.astype(jnp.bfloat16)
    x_parts, y_parts, z_parts = out_ref.shape[:3]
    for y in range(y_parts):
        for z in range(z_parts):
            for x in range(0, x_parts, 2):
                first = ((y * z_parts + z) * x_parts + x) * HEAD_DIM
                cols = jnp.dot(rows, weight_ref[:, first : first + 2 * HEAD_DIM], preferred_element_type=jnp.float32)
                cols = cols.astype(jnp.bfloat16)
                out_ref[x, y, z] = cols[:, :HEAD_DIM]
                out_ref[x + 1, y, z] = cols[:, HEAD_DIM:]


def sum_body(parts_ref, out_ref):
    for y in range(out_ref.shape[0]):
        for z in range(out_ref.shape[1]):
            out_ref[y, z] = functools.reduce(
                jnp.add, [parts_ref[i, y, z].astype(jnp.float32) for i in range(parts_ref.shape[0])]
            ).astype(jnp.bfloat16)


def split_sum_body(parts_ref, own_ref, cross_ref):
    z = lax.axis_index("z")
    for ref, half in ((cross_ref, 1 - z), (own_ref, z)):
        ref[...] = functools.reduce(
            jnp.add, [parts_ref[i, half].astype(jnp.float32) for i in range(parts_ref.shape[0])]
        ).astype(jnp.bfloat16)


def add_body(own_ref, other_ref, out_ref):
    out_ref[...] = (own_ref[...].astype(jnp.float32) + other_ref[...].astype(jnp.float32)).astype(jnp.bfloat16)


def shape(*dims):
    return jax.ShapeDtypeStruct(dims, jnp.bfloat16)


def on_device(queries, keys, values, lengths, selected, out_weight):
    rows = queries.shape[0]
    segments, z_parts, x_parts, y_parts = (lax.axis_size(a) for a in ("segment", "z", "x", "head"))
    message = HEAD_DIM + STAT_ROWS
    tile = (rows, HEAD_DIM)

    partial_terms = pl.pallas_call(
        functools.partial(attend_body, together=2),
        out_shape=shape(x_parts, z_parts, message, rows),
        in_specs=[pl.BlockSpec(memory_space=pltpu.SMEM)] * 2 + whole(3),
        out_specs=whole(1)[0],
        scratch_shapes=[pltpu.VMEM((HEAD_DIM, keys.shape[0]), jnp.bfloat16)],
        name="attend",
    )(lengths, selected, queries, keys, values)
    partial_terms = lax.all_to_all(partial_terms, "x", 0, 0, tiled=True)
    own, cross = pl.pallas_call(
        merge_body,
        out_shape=[shape(message, rows)] * 2,
        in_specs=whole(1),
        out_specs=whole(2),
        name="merge",
    )(partial_terms)
    swap = [(z, z_parts - 1 - z) for z in range(z_parts)]
    other = lax.ppermute(cross, "z", swap)
    products = pl.pallas_call(
        project_body,
        out_shape=shape(x_parts, y_parts, z_parts, *tile),
        in_specs=whole(3),
        out_specs=whole(1)[0],
        name="project",
    )(own, other, out_weight)
    products = lax.all_to_all(products, "x", 0, 0, tiled=True)
    products = pl.pallas_call(
        sum_body,
        out_shape=shape(y_parts, z_parts, *tile),
        in_specs=whole(1),
        out_specs=whole(1)[0],
        name="sum_x",
    )(products)
    products = lax.all_to_all(products, "head", 0, 0, tiled=True)
    own, cross = pl.pallas_call(
        split_sum_body,
        out_shape=[shape(*tile)] * 2,
        in_specs=whole(1),
        out_specs=whole(2),
        name="sum_y",
    )(products)

    def onward(part, flip):
        pairs = [
            (s * z_parts + z, (s + 1) % segments * z_parts + (z ^ flip))
            for s in range(segments)
            for z in range(z_parts)
        ]
        return lax.ppermute(part, ("segment", "z"), pairs)

    other = onward(cross, 1)
    own = onward(own, 0)
    return pl.pallas_call(
        add_body,
        out_shape=shape(*tile),
        in_specs=whole(2),
        out_specs=whole(1)[0],
        name="sum_z",
    )(own, other)


def solution(mesh):
    segment, ctx, head = mesh.devices.shape
    split = jax.sharding.Mesh(
        mesh.devices.reshape(segment, Z_PARTS, ctx // Z_PARTS, head), ("segment", "z", "x", "head")
    )
    sections = ("segment", "z", "x")
    placed = (
        P("segment", "head"),
        P(sections, "head"),
        P(sections, "head"),
        P("segment"),
        P("segment", None),
        P(("head", "z", "x"), None),
    )
    return jax.shard_map(
        on_device,
        mesh=split,
        in_specs=placed,
        out_specs=P("segment", ("head", "z", "x")),
        check_vma=False,
    )
```

```python
import functools
import math

import jax
import jax.numpy as jnp
from jax import lax
from jax.experimental import pallas as pl
from jax.experimental.pallas import tpu as pltpu
from jax.sharding import PartitionSpec as P


HEAD_DIM = 128
STAT_ROWS = 16
MASKED = -1e30
LOG2E = 1.4426950408889634
Z_PARTS = 2


def whole(count):
    return [pl.BlockSpec(memory_space=pltpu.VMEM)] * count


def stat_rows(lse):
    high = lse.astype(jnp.bfloat16).astype(jnp.float32)
    rest = lse - high
    mid = rest.astype(jnp.bfloat16).astype(jnp.float32)
    low = rest - mid
    row = lax.broadcasted_iota(jnp.int32, (STAT_ROWS, lse.shape[1]), 0)
    return jnp.where(row == 0, high, jnp.where(row == 1, mid, low)).astype(jnp.bfloat16)


def pack_body(weight_ref, out_ref, held, loads, stores):
    x_parts = out_ref.shape[0]
    places = weight_ref.shape[1] // HEAD_DIM // x_parts

    def load(x, place):
        first = (place * x_parts + x) * HEAD_DIM
        return pltpu.make_async_copy(
            weight_ref.at[:, first : first + HEAD_DIM],
            held.at[x, :, place * HEAD_DIM : (place + 1) * HEAD_DIM],
            loads.at[x, place],
        )

    def store(x):
        return pltpu.make_async_copy(held.at[x], out_ref.at[x], stores.at[x])

    for x in range(x_parts):
        for place in range(places):
            load(x, place).start()
    for x in range(x_parts):
        for place in range(places):
            load(x, place).wait()
        store(x).start()
    for x in range(x_parts):
        store(x).wait()


def attend_body(cached_ref, chosen_ref, q_ref, k_ref, v_ref, own_ref, cross_ref, vt_ref, together):
    x_parts = own_ref.shape[0]
    rows = q_ref.shape[0]
    span = k_ref.shape[0]
    z = lax.axis_index("z")
    block_id = z * x_parts + lax.axis_index("x")
    usable = cached_ref[0] - block_id * span
    named = chosen_ref[0, 0] == block_id
    for i in range(1, chosen_ref.shape[1]):
        named = jnp.logical_or(named, chosen_ref[0, i] == block_id)
    picked = jnp.logical_and(usable > 0, named)
    factor = LOG2E / math.sqrt(HEAD_DIM)

    @pl.when(jnp.logical_not(picked))
    def _():
        for ref in (cross_ref, own_ref):
            for x in range(x_parts):
                ref[x, :HEAD_DIM, :] = jnp.zeros((HEAD_DIM, rows), jnp.bfloat16)
                ref[x, HEAD_DIM:, :] = jnp.full((STAT_ROWS, rows), MASKED, jnp.bfloat16)

    def compute(masked):
        vt_ref[...] = v_ref[...].T
        for ref, side in ((cross_ref, 1 - z), (own_ref, z)):
            for x in range(0, x_parts, together):
                first = pl.multiple_of((side * x_parts + x) * HEAD_DIM, HEAD_DIM)
                heads = q_ref[:, pl.ds(first, together * HEAD_DIM)]
                scores = lax.dot_general(
                    k_ref[...],
                    jnp.concatenate([heads[:, i * HEAD_DIM : (i + 1) * HEAD_DIM] for i in range(together)], axis=0),
                    (((1,), (1,)), ((), ())),
                    preferred_element_type=jnp.float32,
                )
                if masked:
                    position = lax.broadcasted_iota(jnp.int32, scores.shape, 0)
                    scores = jnp.where(position < usable, scores, MASKED)
                top = jnp.max(scores, axis=0, keepdims=True)
                expo = jnp.exp2((scores - top) * factor)
                total = jnp.sum(expo, axis=0, keepdims=True)
                gathered = jnp.dot(vt_ref[...], expo.astype(jnp.bfloat16), preferred_element_type=jnp.float32)
                gathered = (gathered / total).astype(jnp.bfloat16)
                stats = stat_rows(top * factor + jnp.log2(total))
                for i in range(together):
                    ref[x + i, :HEAD_DIM, :] = gathered[:, i * rows : (i + 1) * rows]
                    ref[x + i, HEAD_DIM:, :] = stats[:, i * rows : (i + 1) * rows]

    pl.when(jnp.logical_and(picked, usable >= span))(lambda: compute(False))
    pl.when(jnp.logical_and(picked, usable < span))(lambda: compute(True))


def merged(parts):
    logs = []
    for part in parts:
        stats = part[HEAD_DIM:, :].astype(jnp.float32)
        logs.append(stats[0:1] + stats[1:2] + stats[2:3])
    top = functools.reduce(jnp.maximum, logs)
    shares = [jnp.exp2(log - top) for log in logs]
    total = functools.reduce(jnp.add, shares)
    summed = functools.reduce(
        jnp.add, [part[:HEAD_DIM, :].astype(jnp.float32) * (share / total) for part, share in zip(parts, shares)]
    )
    return summed, top + jnp.log2(total)


def merge_body(own_ref, other_ref, out_ref):
    for head in range(own_ref.shape[0]):
        out, log = merged([own_ref[head], other_ref[head]])
        out = out.astype(jnp.bfloat16)
        log = stat_rows(log)
        for x in range(out_ref.shape[0]):
            out_ref[x, head, :HEAD_DIM, :] = out
            out_ref[x, head, HEAD_DIM:, :] = log


def project_body(parts_ref, weight_ref, out_ref):
    heads = []
    for head in range(parts_ref.shape[1]):
        out, _ = merged([parts_ref[i, head] for i in range(parts_ref.shape[0])])
        heads.append(out.astype(jnp.bfloat16).T)
    rows = jnp.concatenate(heads, axis=1)
    y_parts, z_parts = out_ref.shape[:2]
    for y in range(y_parts):
        first = y * z_parts * HEAD_DIM
        block = weight_ref[:, :, first : first + z_parts * HEAD_DIM].reshape(-1, z_parts * HEAD_DIM)
        cols = jnp.dot(rows, block, preferred_element_type=jnp.float32).astype(jnp.bfloat16)
        for z in range(z_parts):
            out_ref[y, z] = cols[:, z * HEAD_DIM : (z + 1) * HEAD_DIM]


def split_sum_body(parts_ref, own_ref, cross_ref):
    z = lax.axis_index("z")
    for ref, half in ((cross_ref, 1 - z), (own_ref, z)):
        ref[...] = functools.reduce(
            jnp.add, [parts_ref[i, half].astype(jnp.float32) for i in range(parts_ref.shape[0])]
        ).astype(jnp.bfloat16)


def shape(*dims):
    return jax.ShapeDtypeStruct(dims, jnp.bfloat16)


def on_device(queries, keys, values, lengths, selected, out_weight):
    rows = queries.shape[0]
    segments, z_parts, x_parts, y_parts = (lax.axis_size(a) for a in ("segment", "z", "x", "head"))
    message = HEAD_DIM + STAT_ROWS
    tile = (rows, HEAD_DIM)

    def kernel(body, inputs, outputs, mib, **more):
        return pl.pallas_call(
            body,
            out_shape=outputs,
            in_specs=inputs,
            out_specs=whole(len(outputs)),
            compiler_params=pltpu.CompilerParams(vmem_limit_bytes=mib << 20),
            **more,
        )

    packed = out_weight.shape[1] // x_parts
    pack = pl.pallas_call(
        pack_body,
        out_shape=shape(x_parts, HEAD_DIM, packed),
        in_specs=[pl.BlockSpec(memory_space=pl.ANY)],
        out_specs=pl.BlockSpec(memory_space=pl.ANY),
        scratch_shapes=[
            pltpu.VMEM((x_parts, HEAD_DIM, packed), jnp.bfloat16),
            pltpu.SemaphoreType.DMA((x_parts, packed // HEAD_DIM)),
            pltpu.SemaphoreType.DMA((x_parts,)),
        ],
        name="pack",
    )(out_weight)
    weight = lax.all_to_all(pack, "x", 0, 0, tiled=True)
    own, cross = kernel(
        functools.partial(attend_body, together=4),
        [pl.BlockSpec(memory_space=pltpu.SMEM)] * 2 + whole(3),
        [shape(x_parts, message, rows)] * 2,
        32,
        scratch_shapes=[
            pltpu.VMEM((HEAD_DIM, keys.shape[0]), jnp.bfloat16),
        ],
    )(lengths, selected, queries, keys, values)
    swap = [(z, z_parts - 1 - z) for z in range(z_parts)]
    other = lax.ppermute(cross, "z", swap)
    (terms,) = kernel(merge_body, whole(2), [shape(x_parts, x_parts, message, rows)], 8)(own, other)
    terms = lax.all_to_all(terms, "x", 0, 0, tiled=True)
    (products,) = kernel(project_body, whole(2), [shape(y_parts, z_parts, *tile)], 16)(terms, weight)
    products = lax.all_to_all(products, "head", 0, 0, tiled=True)
    own, cross = kernel(split_sum_body, whole(1), [shape(*tile)] * 2, 8)(products)

    def onward(part, flip):
        pairs = [
            (s * z_parts + z, (s + 1) % segments * z_parts + (z ^ flip))
            for s in range(segments)
            for z in range(z_parts)
        ]
        return lax.ppermute(part, ("segment", "z"), pairs)

    other = onward(cross, 1)
    own = onward(own, 0)
    return (own.astype(jnp.float32) + other.astype(jnp.float32)).astype(jnp.bfloat16)


def solution(mesh):
    segment, ctx, head = mesh.devices.shape
    split = jax.sharding.Mesh(
        mesh.devices.reshape(segment, Z_PARTS, ctx // Z_PARTS, head), ("segment", "z", "x", "head")
    )
    sections = ("segment", "z", "x")
    placed = (
        P("segment", "head"),
        P(sections, "head"),
        P(sections, "head"),
        P("segment"),
        P("segment", None),
        P(("head", "z", "x"), None),
    )
    return jax.shard_map(
        on_device,
        mesh=split,
        in_specs=placed,
        out_specs=P("segment", ("head", "z", "x")),
        check_vma=False,
    )
```

```python
import functools
import math

import jax
import jax.numpy as jnp
from jax import lax
from jax.experimental import pallas as pl
from jax.experimental.pallas import tpu as pltpu
from jax.sharding import PartitionSpec as P


HEAD_DIM = 128
STAT_ROWS = 16
MASKED = -1e30
LOG2E = 1.4426950408889634
Z_PARTS = 2
CORES = 2


def whole(count):
    return [pl.BlockSpec(memory_space=pltpu.VMEM)] * count


def stat_rows(lse):
    high = lse.astype(jnp.bfloat16).astype(jnp.float32)
    rest = lse - high
    mid = rest.astype(jnp.bfloat16).astype(jnp.float32)
    low = rest - mid
    row = lax.broadcasted_iota(jnp.int32, (STAT_ROWS, lse.shape[1]), 0)
    return jnp.where(row == 0, high, jnp.where(row == 1, mid, low)).astype(jnp.bfloat16)


def pack_body(weight_ref, out_ref, held, loads, stores):
    x_parts = out_ref.shape[0]
    places = out_ref.shape[2] // HEAD_DIM
    core = lax.axis_index("segment") % CORES

    def load(x, place):
        first = pl.multiple_of(((core * places + place) * x_parts + x) * HEAD_DIM, HEAD_DIM)
        return pltpu.make_async_copy(
            weight_ref.at[:, pl.ds(first, HEAD_DIM)],
            held.at[x, :, place * HEAD_DIM : (place + 1) * HEAD_DIM],
            loads.at[x, place],
        )

    def store(x):
        return pltpu.make_async_copy(held.at[x], out_ref.at[x], stores.at[x])

    for x in range(x_parts):
        for place in range(places):
            load(x, place).start()
    for x in range(x_parts):
        for place in range(places):
            load(x, place).wait()
        store(x).start()
    for x in range(x_parts):
        store(x).wait()


def attend_body(cached_ref, chosen_ref, q_ref, k_ref, v_ref, own_ref, cross_ref, vt_ref, together):
    x_parts = own_ref.shape[0]
    rows = q_ref.shape[0]
    span = k_ref.shape[0]
    z = lax.axis_index("z")
    block_id = z * x_parts + lax.axis_index("x")
    usable = cached_ref[0] - block_id * span
    named = chosen_ref[0, 0] == block_id
    for i in range(1, chosen_ref.shape[1]):
        named = jnp.logical_or(named, chosen_ref[0, i] == block_id)
    picked = jnp.logical_and(usable > 0, named)
    factor = LOG2E / math.sqrt(HEAD_DIM)

    @pl.when(jnp.logical_not(picked))
    def _():
        for ref in (cross_ref, own_ref):
            for x in range(x_parts):
                ref[x, :HEAD_DIM, :] = jnp.zeros((HEAD_DIM, rows), jnp.bfloat16)
                ref[x, HEAD_DIM:, :] = jnp.full((STAT_ROWS, rows), MASKED, jnp.bfloat16)

    def compute(masked):
        vt_ref[...] = v_ref[...].T
        for ref, side in ((cross_ref, 1 - z), (own_ref, z)):
            for x in range(0, x_parts, together):
                first = pl.multiple_of((side * x_parts + x) * HEAD_DIM, HEAD_DIM)
                heads = q_ref[:, pl.ds(first, together * HEAD_DIM)]
                scores = lax.dot_general(
                    k_ref[...],
                    jnp.concatenate([heads[:, i * HEAD_DIM : (i + 1) * HEAD_DIM] for i in range(together)], axis=0),
                    (((1,), (1,)), ((), ())),
                    preferred_element_type=jnp.float32,
                )
                if masked:
                    position = lax.broadcasted_iota(jnp.int32, scores.shape, 0)
                    scores = jnp.where(position < usable, scores, MASKED)
                top = jnp.max(scores, axis=0, keepdims=True)
                expo = jnp.exp2((scores - top) * factor)
                total = jnp.sum(expo, axis=0, keepdims=True)
                gathered = jnp.dot(vt_ref[...], expo.astype(jnp.bfloat16), preferred_element_type=jnp.float32)
                gathered = (gathered / total).astype(jnp.bfloat16)
                stats = stat_rows(top * factor + jnp.log2(total))
                for i in range(together):
                    ref[x + i, :HEAD_DIM, :] = gathered[:, i * rows : (i + 1) * rows]
                    ref[x + i, HEAD_DIM:, :] = stats[:, i * rows : (i + 1) * rows]

    pl.when(jnp.logical_and(picked, usable >= span))(lambda: compute(False))
    pl.when(jnp.logical_and(picked, usable < span))(lambda: compute(True))


def merged(parts):
    logs = []
    for part in parts:
        stats = part[HEAD_DIM:, :].astype(jnp.float32)
        logs.append(stats[0:1] + stats[1:2] + stats[2:3])
    top = functools.reduce(jnp.maximum, logs)
    shares = [jnp.exp2(log - top) for log in logs]
    total = functools.reduce(jnp.add, shares)
    summed = functools.reduce(
        jnp.add, [part[:HEAD_DIM, :].astype(jnp.float32) * (share / total) for part, share in zip(parts, shares)]
    )
    return summed, top + jnp.log2(total)


def merge_body(own_ref, other_ref, out_ref):
    for head in range(own_ref.shape[0]):
        out, log = merged([own_ref[head], other_ref[head]])
        out = out.astype(jnp.bfloat16)
        log = stat_rows(log)
        for x in range(out_ref.shape[0]):
            out_ref[x, head, :HEAD_DIM, :] = out
            out_ref[x, head, HEAD_DIM:, :] = log


def project_body(parts_ref, kept_ref, given_ref, out_ref):
    heads = []
    for head in range(parts_ref.shape[1]):
        out, _ = merged([parts_ref[i, head] for i in range(parts_ref.shape[0])])
        heads.append(out.astype(jnp.bfloat16).T)
    rows = jnp.concatenate(heads, axis=1)
    y_parts, z_parts = out_ref.shape[:2]
    core = lax.axis_index("segment") % CORES
    for half, weight_ref in ((core, kept_ref), (1 - core, given_ref)):
        for y in range(y_parts // CORES):
            first = y * z_parts * HEAD_DIM
            block = weight_ref[:, :, first : first + z_parts * HEAD_DIM].reshape(-1, z_parts * HEAD_DIM)
            cols = jnp.dot(rows, block, preferred_element_type=jnp.float32).astype(jnp.bfloat16)
            for z in range(z_parts):
                out_ref[half * (y_parts // CORES) + y, z] = cols[:, z * HEAD_DIM : (z + 1) * HEAD_DIM]


def split_sum_body(parts_ref, own_ref, cross_ref):
    z = lax.axis_index("z")
    for ref, half in ((cross_ref, 1 - z), (own_ref, z)):
        ref[...] = functools.reduce(
            jnp.add, [parts_ref[i, half].astype(jnp.float32) for i in range(parts_ref.shape[0])]
        ).astype(jnp.bfloat16)


def shape(*dims):
    return jax.ShapeDtypeStruct(dims, jnp.bfloat16)


def on_device(queries, keys, values, lengths, selected, out_weight):
    rows = queries.shape[0]
    segments, z_parts, x_parts, y_parts = (lax.axis_size(a) for a in ("segment", "z", "x", "head"))
    message = HEAD_DIM + STAT_ROWS
    tile = (rows, HEAD_DIM)

    def kernel(body, inputs, outputs, mib, **more):
        return pl.pallas_call(
            body,
            out_shape=outputs,
            in_specs=inputs,
            out_specs=whole(len(outputs)),
            compiler_params=pltpu.CompilerParams(vmem_limit_bytes=mib << 20),
            **more,
        )

    packed = out_weight.shape[1] // x_parts // CORES
    pack = pl.pallas_call(
        pack_body,
        out_shape=shape(x_parts, HEAD_DIM, packed),
        in_specs=[pl.BlockSpec(memory_space=pl.ANY)],
        out_specs=pl.BlockSpec(memory_space=pl.ANY),
        scratch_shapes=[
            pltpu.VMEM((x_parts, HEAD_DIM, packed), jnp.bfloat16),
            pltpu.SemaphoreType.DMA((x_parts, packed // HEAD_DIM)),
            pltpu.SemaphoreType.DMA((x_parts,)),
        ],
        name="pack",
    )(out_weight)
    weight = lax.all_to_all(pack, "x", 0, 0, tiled=True)
    own, cross = kernel(
        functools.partial(attend_body, together=4),
        [pl.BlockSpec(memory_space=pltpu.SMEM)] * 2 + whole(3),
        [shape(x_parts, message, rows)] * 2,
        32,
        scratch_shapes=[
            pltpu.VMEM((HEAD_DIM, keys.shape[0]), jnp.bfloat16),
        ],
    )(lengths, selected, queries, keys, values)

    def onward(part, flip):
        pairs = [
            (s * z_parts + z, (s + 1) % segments * z_parts + (z ^ flip))
            for s in range(segments)
            for z in range(z_parts)
        ]
        return lax.ppermute(part, ("segment", "z"), pairs)

    other = onward(cross, 1)
    own = onward(own, 0)
    given = lax.ppermute(weight, "segment", [(s, s ^ 1) for s in range(segments)])
    (terms,) = kernel(merge_body, whole(2), [shape(x_parts, x_parts, message, rows)], 8)(own, other)
    terms = lax.all_to_all(terms, "x", 0, 0, tiled=True)
    (products,) = kernel(project_body, whole(3), [shape(y_parts, z_parts, *tile)], 16)(terms, weight, given)
    products = lax.all_to_all(products, "head", 0, 0, tiled=True)
    own, cross = kernel(split_sum_body, whole(1), [shape(*tile)] * 2, 8)(products)

    other = lax.ppermute(cross, "z", [(z, z_parts - 1 - z) for z in range(z_parts)])
    return (own.astype(jnp.float32) + other.astype(jnp.float32)).astype(jnp.bfloat16)


def solution(mesh):
    segment, ctx, head = mesh.devices.shape
    split = jax.sharding.Mesh(
        mesh.devices.reshape(segment, Z_PARTS, ctx // Z_PARTS, head), ("segment", "z", "x", "head")
    )
    sections = ("segment", "z", "x")
    placed = (
        P("segment", "head"),
        P(sections, "head"),
        P(sections, "head"),
        P("segment"),
        P("segment", None),
        P(("head", "z", "x"), None),
    )
    return jax.shard_map(
        on_device,
        mesh=split,
        in_specs=placed,
        out_specs=P("segment", ("head", "z", "x")),
        check_vma=False,
    )
```

```python
import functools
import math

import jax
import jax.numpy as jnp
from jax import lax
from jax.experimental import pallas as pl
from jax.experimental.pallas import tpu as pltpu
from jax.sharding import PartitionSpec as P


HEAD_DIM = 128
STAT_ROWS = 16
MASKED = -1e30
LOG2E = 1.4426950408889634
Z_PARTS = 2
CORES = 2


def whole(count):
    return [pl.BlockSpec(memory_space=pltpu.VMEM)] * count


def stat_rows(logs):
    pieces = []
    for log in logs:
        high = log.astype(jnp.bfloat16).astype(jnp.float32)
        mid = (log - high).astype(jnp.bfloat16).astype(jnp.float32)
        pieces += [high, mid, log - high - mid]
    index = lax.broadcasted_iota(jnp.int32, (STAT_ROWS, logs[0].shape[1]), 0)
    rows = jnp.zeros(index.shape, jnp.float32)
    for i, piece in enumerate(pieces):
        rows = jnp.where(index == i, piece, rows)
    return rows.astype(jnp.bfloat16)


def outs_and_logs(block):
    count = block.shape[0] // HEAD_DIM
    stats = block[count * HEAD_DIM :, :].astype(jnp.float32)
    outs = [block[i * HEAD_DIM : (i + 1) * HEAD_DIM, :].astype(jnp.float32) for i in range(count)]
    return outs, [stats[3 * i : 3 * i + 1] + stats[3 * i + 1 : 3 * i + 2] + stats[3 * i + 2 : 3 * i + 3] for i in range(count)]


def pack_body(weight_ref, out_ref, held, loads, stores):
    x_parts = out_ref.shape[0]
    places = out_ref.shape[2] // HEAD_DIM
    core = lax.axis_index("segment") % CORES

    def load(x, place):
        first = pl.multiple_of(((core * places + place) * x_parts + x) * HEAD_DIM, HEAD_DIM)
        return pltpu.make_async_copy(
            weight_ref.at[:, pl.ds(first, HEAD_DIM)],
            held.at[x, :, place * HEAD_DIM : (place + 1) * HEAD_DIM],
            loads.at[x, place],
        )

    def store(x):
        return pltpu.make_async_copy(held.at[x], out_ref.at[x], stores.at[x])

    for x in range(x_parts):
        for place in range(places):
            load(x, place).start()
    for x in range(x_parts):
        for place in range(places):
            load(x, place).wait()
        store(x).start()
    for x in range(x_parts):
        store(x).wait()


def attend_body(cached_ref, chosen_ref, q_ref, k_ref, v_ref, own_ref, cross_ref, vt_ref):
    x_parts = own_ref.shape[0] // HEAD_DIM
    rows = q_ref.shape[0]
    span = k_ref.shape[0]
    z = lax.axis_index("z")
    block_id = z * x_parts + lax.axis_index("x")
    usable = cached_ref[0] - block_id * span
    named = chosen_ref[0, 0] == block_id
    for i in range(1, chosen_ref.shape[1]):
        named = jnp.logical_or(named, chosen_ref[0, i] == block_id)
    picked = jnp.logical_and(usable > 0, named)
    factor = LOG2E / math.sqrt(HEAD_DIM)

    @pl.when(jnp.logical_not(picked))
    def _():
        for ref in (cross_ref, own_ref):
            ref[: x_parts * HEAD_DIM, :] = jnp.zeros((x_parts * HEAD_DIM, rows), jnp.bfloat16)
            ref[x_parts * HEAD_DIM :, :] = jnp.full((STAT_ROWS, rows), MASKED, jnp.bfloat16)

    def compute(masked):
        vt_ref[...] = v_ref[...].T
        for ref, side in ((cross_ref, 1 - z), (own_ref, z)):
            first = pl.multiple_of(side * x_parts * HEAD_DIM, HEAD_DIM)
            heads = q_ref[:, pl.ds(first, x_parts * HEAD_DIM)]
            scores = lax.dot_general(
                k_ref[...],
                jnp.concatenate([heads[:, i * HEAD_DIM : (i + 1) * HEAD_DIM] for i in range(x_parts)], axis=0),
                (((1,), (1,)), ((), ())),
                preferred_element_type=jnp.float32,
            )
            if masked:
                position = lax.broadcasted_iota(jnp.int32, scores.shape, 0)
                scores = jnp.where(position < usable, scores, MASKED)
            top = jnp.max(scores, axis=0, keepdims=True)
            expo = jnp.exp2((scores - top) * factor)
            total = jnp.sum(expo, axis=0, keepdims=True)
            gathered = jnp.dot(vt_ref[...], expo.astype(jnp.bfloat16), preferred_element_type=jnp.float32)
            gathered = (gathered / total).astype(jnp.bfloat16)
            logs = top * factor + jnp.log2(total)
            for i in range(x_parts):
                ref[i * HEAD_DIM : (i + 1) * HEAD_DIM, :] = gathered[:, i * rows : (i + 1) * rows]
            ref[x_parts * HEAD_DIM :, :] = stat_rows([logs[:, i * rows : (i + 1) * rows] for i in range(x_parts)])

    pl.when(jnp.logical_and(picked, usable >= span))(lambda: compute(False))
    pl.when(jnp.logical_and(picked, usable < span))(lambda: compute(True))


def merged(outs, logs):
    top = functools.reduce(jnp.maximum, logs)
    shares = [jnp.exp2(log - top) for log in logs]
    total = functools.reduce(jnp.add, shares)
    summed = functools.reduce(jnp.add, [out * (share / total) for out, share in zip(outs, shares)])
    return summed, top + jnp.log2(total)


def merge_body(own_ref, other_ref, out_ref):
    absent = jnp.logical_and(lax.axis_index("segment") % 2 == 0, lax.axis_index("z") == 0)
    own, own_logs = outs_and_logs(own_ref[...])
    other, other_logs = outs_and_logs(other_ref[...])
    logs = []
    for head in range(len(own)):
        there = jnp.where(absent, MASKED, other_logs[head])
        out, log = merged([own[head], other[head]], [own_logs[head], there])
        out = out.astype(jnp.bfloat16)
        for x in range(out_ref.shape[0]):
            out_ref[x, head * HEAD_DIM : (head + 1) * HEAD_DIM, :] = out
        logs.append(log)
    stats = stat_rows(logs)
    for x in range(out_ref.shape[0]):
        out_ref[x, len(own) * HEAD_DIM :, :] = stats


def project_body(parts_ref, kept_ref, given_ref, out_ref):
    parts = [outs_and_logs(parts_ref[i]) for i in range(parts_ref.shape[0])]
    heads = []
    for head in range(len(parts[0][0])):
        out, _ = merged([outs[head] for outs, _ in parts], [logs[head] for _, logs in parts])
        heads.append(out.astype(jnp.bfloat16).T)
    rows = jnp.concatenate(heads, axis=1)
    y_parts, z_parts = out_ref.shape[:2]
    core = lax.axis_index("segment") % CORES
    for half, weight_ref in ((core, kept_ref), (1 - core, given_ref)):
        for y in range(y_parts // CORES):
            first = y * z_parts * HEAD_DIM
            block = weight_ref[:, :, first : first + z_parts * HEAD_DIM].reshape(-1, z_parts * HEAD_DIM)
            cols = jnp.dot(rows, block, preferred_element_type=jnp.float32).astype(jnp.bfloat16)
            for z in range(z_parts):
                out_ref[half * (y_parts // CORES) + y, z] = cols[:, z * HEAD_DIM : (z + 1) * HEAD_DIM]


def split_sum_body(parts_ref, own_ref, cross_ref):
    z = lax.axis_index("z")
    for ref, half in ((cross_ref, 1 - z), (own_ref, z)):
        ref[...] = functools.reduce(
            jnp.add, [parts_ref[i, half].astype(jnp.float32) for i in range(parts_ref.shape[0])]
        ).astype(jnp.bfloat16)


def shape(*dims):
    return jax.ShapeDtypeStruct(dims, jnp.bfloat16)


def on_device(queries, keys, values, lengths, selected, out_weight):
    rows = queries.shape[0]
    segments, z_parts, x_parts, y_parts = (lax.axis_size(a) for a in ("segment", "z", "x", "head"))
    message = x_parts * HEAD_DIM + STAT_ROWS
    tile = (rows, HEAD_DIM)

    def kernel(body, inputs, outputs, mib, **more):
        return pl.pallas_call(
            body,
            out_shape=outputs,
            in_specs=inputs,
            out_specs=whole(len(outputs)),
            compiler_params=pltpu.CompilerParams(vmem_limit_bytes=mib << 20),
            **more,
        )

    packed = out_weight.shape[1] // x_parts // CORES
    pack = pl.pallas_call(
        pack_body,
        out_shape=shape(x_parts, HEAD_DIM, packed),
        in_specs=[pl.BlockSpec(memory_space=pl.ANY)],
        out_specs=pl.BlockSpec(memory_space=pl.ANY),
        scratch_shapes=[
            pltpu.VMEM((x_parts, HEAD_DIM, packed), jnp.bfloat16),
            pltpu.SemaphoreType.DMA((x_parts, packed // HEAD_DIM)),
            pltpu.SemaphoreType.DMA((x_parts,)),
        ],
        name="pack",
    )(out_weight)
    weight = lax.all_to_all(pack, "x", 0, 0, tiled=True)
    own, cross = kernel(
        attend_body,
        [pl.BlockSpec(memory_space=pltpu.SMEM)] * 2 + whole(3),
        [shape(message, rows)] * 2,
        32,
        scratch_shapes=[
            pltpu.VMEM((HEAD_DIM, keys.shape[0]), jnp.bfloat16),
        ],
    )(lengths, selected, queries, keys, values)

    def onward(part, flip):
        pairs = [
            (s * z_parts + z, (s + 1) % segments * z_parts + (z ^ flip))
            for s in range(segments)
            for z in range(z_parts)
        ]
        return lax.ppermute(part, ("segment", "z"), pairs)

    swap = [(s * z_parts + z, s * z_parts + 1 - z) for s in range(segments) for z in range(z_parts) if s % 2 or z == 0]
    other = lax.ppermute(cross, ("segment", "z"), swap)
    given = lax.ppermute(weight, "segment", [(s, s ^ 1) for s in range(segments)])
    (terms,) = kernel(merge_body, whole(2), [shape(x_parts, message, rows)], 8)(own, other)
    terms = lax.all_to_all(terms, "x", 0, 0, tiled=True)
    (products,) = kernel(project_body, whole(3), [shape(y_parts, z_parts, *tile)], 16)(terms, weight, given)
    products = lax.all_to_all(products, "head", 0, 0, tiled=True)
    own, cross = kernel(split_sum_body, whole(1), [shape(*tile)] * 2, 8)(products)

    other = onward(cross, 1)
    own = onward(own, 0)
    return (own.astype(jnp.float32) + other.astype(jnp.float32)).astype(jnp.bfloat16)


def solution(mesh):
    segment, ctx, head = mesh.devices.shape
    split = jax.sharding.Mesh(
        mesh.devices.reshape(segment, Z_PARTS, ctx // Z_PARTS, head), ("segment", "z", "x", "head")
    )
    sections = ("segment", "z", "x")
    placed = (
        P("segment", "head"),
        P(sections, "head"),
        P(sections, "head"),
        P("segment"),
        P("segment", None),
        P(("head", "z", "x"), None),
    )
    return jax.shard_map(
        on_device,
        mesh=split,
        in_specs=placed,
        out_specs=P("segment", ("head", "z", "x")),
        check_vma=False,
    )
```

```python
import functools
import math

import jax
import jax.numpy as jnp
from jax import lax
from jax.experimental import pallas as pl
from jax.experimental.pallas import tpu as pltpu
from jax.sharding import PartitionSpec as P


HEAD_DIM = 128
STAT_ROWS = 16
MASKED = -1e30
LOG2E = 1.4426950408889634
Z_PARTS = 2
CORES = 2


def whole(count):
    return [pl.BlockSpec(memory_space=pltpu.VMEM)] * count


def stat_rows(logs):
    pieces = []
    for log in logs:
        high = log.astype(jnp.bfloat16).astype(jnp.float32)
        mid = (log - high).astype(jnp.bfloat16).astype(jnp.float32)
        pieces += [high, mid, log - high - mid]
    index = lax.broadcasted_iota(jnp.int32, (STAT_ROWS, logs[0].shape[1]), 0)
    rows = jnp.zeros(index.shape, jnp.float32)
    for i, piece in enumerate(pieces):
        rows = jnp.where(index == i, piece, rows)
    return rows.astype(jnp.bfloat16)


def outs_and_logs(block):
    count = block.shape[0] // HEAD_DIM
    stats = block[count * HEAD_DIM :, :].astype(jnp.float32)
    outs = [block[i * HEAD_DIM : (i + 1) * HEAD_DIM, :].astype(jnp.float32) for i in range(count)]
    return outs, [stats[3 * i : 3 * i + 1] + stats[3 * i + 1 : 3 * i + 2] + stats[3 * i + 2 : 3 * i + 3] for i in range(count)]


def attend_body(cached_ref, chosen_ref, q_hbm, k_hbm, v_hbm, weight_ref, own_ref, cross_ref, pack_ref, *scratch):
    q_ref, k_ref, v_ref, vt_ref, held, fetches, loads, stores = scratch
    x_parts = own_ref.shape[0] // HEAD_DIM
    rows = q_ref.shape[0]
    span = k_ref.shape[0]
    z = lax.axis_index("z")
    block_id = z * x_parts + lax.axis_index("x")
    usable = cached_ref[0] - block_id * span
    named = chosen_ref[0, 0] == block_id
    for i in range(1, chosen_ref.shape[1]):
        named = jnp.logical_or(named, chosen_ref[0, i] == block_id)
    picked = jnp.logical_and(usable > 0, named)
    factor = LOG2E / math.sqrt(HEAD_DIM)
    pairs = ((q_hbm, q_ref), (k_hbm, k_ref), (v_hbm, v_ref))
    fetch = [pltpu.make_async_copy(*pair, fetches.at[i]) for i, pair in enumerate(pairs)]

    @pl.when(picked)
    def _():
        for copy in fetch:
            copy.start()

    places = pack_ref.shape[2] // HEAD_DIM
    core = lax.axis_index("segment") % CORES

    def load(x, place):
        first = pl.multiple_of(((core * places + place) * x_parts + x) * HEAD_DIM, HEAD_DIM)
        return pltpu.make_async_copy(
            weight_ref.at[:, pl.ds(first, HEAD_DIM)],
            held.at[x, :, place * HEAD_DIM : (place + 1) * HEAD_DIM],
            loads.at[x, place],
        )

    def store(x):
        return pltpu.make_async_copy(held.at[x], pack_ref.at[x], stores.at[x])

    for x in range(x_parts):
        for place in range(places):
            load(x, place).start()

    def pass_on():
        for x in range(x_parts):
            for place in range(places):
                load(x, place).wait()
            store(x).start()

    @pl.when(jnp.logical_not(picked))
    def _():
        for ref in (cross_ref, own_ref):
            ref[: x_parts * HEAD_DIM, :] = jnp.zeros((x_parts * HEAD_DIM, rows), jnp.bfloat16)
            ref[x_parts * HEAD_DIM :, :] = jnp.full((STAT_ROWS, rows), MASKED, jnp.bfloat16)
        pass_on()

    def compute(ref, side, masked):
        first = pl.multiple_of(side * x_parts * HEAD_DIM, HEAD_DIM)
        heads = q_ref[:, pl.ds(first, x_parts * HEAD_DIM)]
        scores = lax.dot_general(
            k_ref[...],
            jnp.concatenate([heads[:, i * HEAD_DIM : (i + 1) * HEAD_DIM] for i in range(x_parts)], axis=0),
            (((1,), (1,)), ((), ())),
            preferred_element_type=jnp.float32,
        )
        if masked:
            position = lax.broadcasted_iota(jnp.int32, scores.shape, 0)
            scores = jnp.where(position < usable, scores, MASKED)
        top = jnp.max(scores, axis=0, keepdims=True)
        expo = jnp.exp2((scores - top) * factor)
        total = jnp.sum(expo, axis=0, keepdims=True)
        gathered = jnp.dot(vt_ref[...], expo.astype(jnp.bfloat16), preferred_element_type=jnp.float32)
        gathered = (gathered / total).astype(jnp.bfloat16)
        logs = top * factor + jnp.log2(total)
        for i in range(x_parts):
            ref[i * HEAD_DIM : (i + 1) * HEAD_DIM, :] = gathered[:, i * rows : (i + 1) * rows]
        ref[x_parts * HEAD_DIM :, :] = stat_rows([logs[:, i * rows : (i + 1) * rows] for i in range(x_parts)])

    def attend(masked):
        for copy in fetch:
            copy.wait()
        vt_ref[...] = v_ref[...].T
        compute(cross_ref, 1 - z, masked)
        pass_on()
        compute(own_ref, z, masked)

    pl.when(jnp.logical_and(picked, usable >= span))(lambda: attend(False))
    pl.when(jnp.logical_and(picked, usable < span))(lambda: attend(True))
    for x in range(x_parts):
        store(x).wait()


def merged(outs, logs):
    top = functools.reduce(jnp.maximum, logs)
    shares = [jnp.exp2(log - top) for log in logs]
    total = functools.reduce(jnp.add, shares)
    summed = functools.reduce(jnp.add, [out * (share / total) for out, share in zip(outs, shares)])
    return summed, top + jnp.log2(total)


def merge_body(own_ref, other_ref, out_ref):
    absent = jnp.logical_and(lax.axis_index("segment") % 2 == 0, lax.axis_index("z") == 0)
    own, own_logs = outs_and_logs(own_ref[...])
    other, other_logs = outs_and_logs(other_ref[...])
    logs = []
    for head in range(len(own)):
        there = jnp.where(absent, MASKED, other_logs[head])
        out, log = merged([own[head], other[head]], [own_logs[head], there])
        out_ref[head * HEAD_DIM : (head + 1) * HEAD_DIM, :] = out.astype(jnp.bfloat16)
        logs.append(log)
    out_ref[len(own) * HEAD_DIM :, :] = stat_rows(logs)


def project_body(*refs):
    terms, (kept_ref, given_ref, out_ref) = refs[:-3], refs[-3:]
    parts = [outs_and_logs(ref[...]) for ref in terms]
    heads = []
    for head in range(len(parts[0][0])):
        out, _ = merged([outs[head] for outs, _ in parts], [logs[head] for _, logs in parts])
        heads.append(out.astype(jnp.bfloat16).T)
    rows = jnp.concatenate(heads, axis=1)
    y_parts, z_parts = out_ref.shape[:2]
    core = lax.axis_index("segment") % CORES
    for half, weight_ref in ((core, kept_ref), (1 - core, given_ref)):
        for y in range(y_parts // CORES):
            first = y * z_parts * HEAD_DIM
            block = weight_ref[:, :, first : first + z_parts * HEAD_DIM].reshape(-1, z_parts * HEAD_DIM)
            cols = jnp.dot(rows, block, preferred_element_type=jnp.float32).astype(jnp.bfloat16)
            for z in range(z_parts):
                out_ref[half * (y_parts // CORES) + y, z] = cols[:, z * HEAD_DIM : (z + 1) * HEAD_DIM]


def split_sum_body(parts_ref, own_ref, cross_ref):
    z = lax.axis_index("z")
    for ref, half in ((cross_ref, 1 - z), (own_ref, z)):
        ref[...] = functools.reduce(
            jnp.add, [parts_ref[i, half].astype(jnp.float32) for i in range(parts_ref.shape[0])]
        ).astype(jnp.bfloat16)


def shape(*dims):
    return jax.ShapeDtypeStruct(dims, jnp.bfloat16)


def on_device(queries, keys, values, lengths, selected, out_weight):
    rows = queries.shape[0]
    segments, z_parts, x_parts, y_parts = (lax.axis_size(a) for a in ("segment", "z", "x", "head"))
    message = x_parts * HEAD_DIM + STAT_ROWS
    tile = (rows, HEAD_DIM)

    def kernel(body, inputs, outputs, mib, **more):
        return pl.pallas_call(
            body,
            out_shape=outputs,
            in_specs=inputs,
            out_specs=whole(len(outputs)),
            compiler_params=pltpu.CompilerParams(vmem_limit_bytes=mib << 20),
            **more,
        )

    packed = out_weight.shape[1] // x_parts // CORES
    places = packed // HEAD_DIM
    vmem = pl.BlockSpec(memory_space=pltpu.VMEM)
    anywhere = pl.BlockSpec(memory_space=pl.ANY)
    own, cross, pack = pl.pallas_call(
        attend_body,
        out_shape=[shape(message, rows)] * 2 + [shape(x_parts, HEAD_DIM, packed)],
        in_specs=[pl.BlockSpec(memory_space=pltpu.SMEM)] * 2 + [anywhere] * 4,
        out_specs=[vmem, vmem, anywhere],
        scratch_shapes=[
            pltpu.VMEM(queries.shape, jnp.bfloat16),
            pltpu.VMEM(keys.shape, jnp.bfloat16),
            pltpu.VMEM(values.shape, jnp.bfloat16),
            pltpu.VMEM((HEAD_DIM, keys.shape[0]), jnp.bfloat16),
            pltpu.VMEM((x_parts, HEAD_DIM, packed), jnp.bfloat16),
            pltpu.SemaphoreType.DMA((3,)),
            pltpu.SemaphoreType.DMA((x_parts, places)),
            pltpu.SemaphoreType.DMA((x_parts,)),
        ],
        name="attend",
    )(lengths, selected, queries, keys, values, out_weight)

    def onward(part, flip):
        pairs = [
            (s * z_parts + z, (s + 1) % segments * z_parts + (z ^ flip))
            for s in range(segments)
            for z in range(z_parts)
        ]
        return lax.ppermute(part, ("segment", "z"), pairs)

    swap = [(s * z_parts + z, s * z_parts + 1 - z) for s in range(segments) for z in range(z_parts) if s % 2 or z == 0]
    other = lax.ppermute(cross, ("segment", "z"), swap)
    kept = lax.all_to_all(pack, "x", 0, 0, tiled=True)
    (terms,) = kernel(merge_body, whole(2), [shape(message, rows)], 8)(own, other)
    shared = [terms]
    for step in sorted(range(1, x_parts), key=lambda k: -min(k, x_parts - k)):
        shared.append(lax.ppermute(terms, "x", [(x, (x + step) % x_parts) for x in range(x_parts)]))
    given = lax.ppermute(kept, "segment", [(s, s ^ 1) for s in range(segments)])
    (products,) = kernel(project_body, whole(x_parts + 2), [shape(y_parts, z_parts, *tile)], 16)(*shared, kept, given)
    products = lax.all_to_all(products, "head", 0, 0, tiled=True)
    own, cross = kernel(split_sum_body, whole(1), [shape(*tile)] * 2, 8)(products)

    other = onward(cross, 1)
    own = onward(own, 0)
    return (own.astype(jnp.float32) + other.astype(jnp.float32)).astype(jnp.bfloat16)


def solution(mesh):
    segment, ctx, head = mesh.devices.shape
    split = jax.sharding.Mesh(
        mesh.devices.reshape(segment, Z_PARTS, ctx // Z_PARTS, head), ("segment", "z", "x", "head")
    )
    sections = ("segment", "z", "x")
    placed = (
        P("segment", "head"),
        P(sections, "head"),
        P(sections, "head"),
        P("segment"),
        P("segment", None),
        P(("head", "z", "x"), None),
    )
    return jax.shard_map(
        on_device,
        mesh=split,
        in_specs=placed,
        out_specs=P("segment", ("head", "z", "x")),
        check_vma=False,
    )
```

```python
import functools
import math

import jax
import jax.numpy as jnp
from jax import lax
from jax.experimental import pallas as pl
from jax.experimental.pallas import tpu as pltpu
from jax.sharding import PartitionSpec as P


HEAD_DIM = 128
STAT_ROWS = 16
MASKED = -1e30
LOG2E = 1.4426950408889634
Z_PARTS = 2
CORES = 2


def whole(count):
    return [pl.BlockSpec(memory_space=pltpu.VMEM)] * count


def stat_rows(logs):
    pieces = []
    for log in logs:
        high = log.astype(jnp.bfloat16).astype(jnp.float32)
        mid = (log - high).astype(jnp.bfloat16).astype(jnp.float32)
        pieces += [high, mid, log - high - mid]
    index = lax.broadcasted_iota(jnp.int32, (STAT_ROWS, logs[0].shape[1]), 0)
    rows = jnp.zeros(index.shape, jnp.float32)
    for i, piece in enumerate(pieces):
        rows = jnp.where(index == i, piece, rows)
    return rows.astype(jnp.bfloat16)


def outs_and_logs(block):
    count = block.shape[0] // HEAD_DIM
    stats = block[count * HEAD_DIM :, :].astype(jnp.float32)
    outs = [block[i * HEAD_DIM : (i + 1) * HEAD_DIM, :].astype(jnp.float32) for i in range(count)]
    return outs, [stats[3 * i : 3 * i + 1] + stats[3 * i + 1 : 3 * i + 2] + stats[3 * i + 2 : 3 * i + 3] for i in range(count)]


def pack_body(weight_ref, out_ref, held, loads, stores):
    x_parts = out_ref.shape[0]
    places = out_ref.shape[2] // HEAD_DIM
    core = lax.axis_index("segment") % CORES

    def load(x, place):
        first = pl.multiple_of(((core * places + place) * x_parts + x) * HEAD_DIM, HEAD_DIM)
        return pltpu.make_async_copy(
            weight_ref.at[:, pl.ds(first, HEAD_DIM)],
            held.at[x, :, place * HEAD_DIM : (place + 1) * HEAD_DIM],
            loads.at[x, place],
        )

    def store(x):
        return pltpu.make_async_copy(held.at[x], out_ref.at[x], stores.at[x])

    for x in range(x_parts):
        for place in range(places):
            load(x, place).start()
    for x in range(x_parts):
        for place in range(places):
            load(x, place).wait()
        store(x).start()
    for x in range(x_parts):
        store(x).wait()


def attend_body(cached_ref, chosen_ref, q_hbm, k_hbm, v_hbm, own_ref, cross_ref, *scratch):
    q_ref, k_ref, v_ref, vt_ref, fetches = scratch
    x_parts = own_ref.shape[0] // HEAD_DIM
    rows = q_ref.shape[0]
    span = k_ref.shape[0]
    z = lax.axis_index("z")
    block_id = z * x_parts + lax.axis_index("x")
    usable = cached_ref[0] - block_id * span
    named = chosen_ref[0, 0] == block_id
    for i in range(1, chosen_ref.shape[1]):
        named = jnp.logical_or(named, chosen_ref[0, i] == block_id)
    picked = jnp.logical_and(usable > 0, named)
    factor = LOG2E / math.sqrt(HEAD_DIM)
    pairs = ((q_hbm, q_ref), (k_hbm, k_ref), (v_hbm, v_ref))
    fetch = [pltpu.make_async_copy(*pair, fetches.at[i]) for i, pair in enumerate(pairs)]

    @pl.when(picked)
    def _():
        for copy in fetch:
            copy.start()

    @pl.when(jnp.logical_not(picked))
    def _():
        for ref in (cross_ref, own_ref):
            ref[: x_parts * HEAD_DIM, :] = jnp.zeros((x_parts * HEAD_DIM, rows), jnp.bfloat16)
            ref[x_parts * HEAD_DIM :, :] = jnp.full((STAT_ROWS, rows), MASKED, jnp.bfloat16)

    def compute(ref, side, masked):
        first = pl.multiple_of(side * x_parts * HEAD_DIM, HEAD_DIM)
        heads = q_ref[:, pl.ds(first, x_parts * HEAD_DIM)]
        scores = lax.dot_general(
            k_ref[...],
            jnp.concatenate([heads[:, i * HEAD_DIM : (i + 1) * HEAD_DIM] for i in range(x_parts)], axis=0),
            (((1,), (1,)), ((), ())),
            preferred_element_type=jnp.float32,
        )
        if masked:
            position = lax.broadcasted_iota(jnp.int32, scores.shape, 0)
            scores = jnp.where(position < usable, scores, MASKED)
        top = jnp.max(scores, axis=0, keepdims=True)
        expo = jnp.exp2((scores - top) * factor)
        total = jnp.sum(expo, axis=0, keepdims=True)
        gathered = jnp.dot(vt_ref[...], expo.astype(jnp.bfloat16), preferred_element_type=jnp.float32)
        gathered = (gathered / total).astype(jnp.bfloat16)
        logs = top * factor + jnp.log2(total)
        for i in range(x_parts):
            ref[i * HEAD_DIM : (i + 1) * HEAD_DIM, :] = gathered[:, i * rows : (i + 1) * rows]
        ref[x_parts * HEAD_DIM :, :] = stat_rows([logs[:, i * rows : (i + 1) * rows] for i in range(x_parts)])

    def attend(masked):
        for copy in fetch:
            copy.wait()
        vt_ref[...] = v_ref[...].T
        compute(cross_ref, 1 - z, masked)
        compute(own_ref, z, masked)

    pl.when(jnp.logical_and(picked, usable >= span))(lambda: attend(False))
    pl.when(jnp.logical_and(picked, usable < span))(lambda: attend(True))


def merged(outs, logs):
    top = functools.reduce(jnp.maximum, logs)
    shares = [jnp.exp2(log - top) for log in logs]
    total = functools.reduce(jnp.add, shares)
    summed = functools.reduce(jnp.add, [out * (share / total) for out, share in zip(outs, shares)])
    return summed, top + jnp.log2(total)


def merge_body(own_ref, other_ref, out_ref):
    absent = jnp.logical_and(lax.axis_index("segment") % 2 == 0, lax.axis_index("z") == 0)
    own, own_logs = outs_and_logs(own_ref[...])
    other, other_logs = outs_and_logs(other_ref[...])
    logs = []
    for head in range(len(own)):
        there = jnp.where(absent, MASKED, other_logs[head])
        out, log = merged([own[head], other[head]], [own_logs[head], there])
        out_ref[head * HEAD_DIM : (head + 1) * HEAD_DIM, :] = out.astype(jnp.bfloat16)
        logs.append(log)
    out_ref[len(own) * HEAD_DIM :, :] = stat_rows(logs)


def project_body(*refs):
    terms, (kept_ref, given_ref, out_ref) = refs[:-3], refs[-3:]
    parts = [outs_and_logs(ref[...]) for ref in terms]
    heads = []
    for head in range(len(parts[0][0])):
        out, _ = merged([outs[head] for outs, _ in parts], [logs[head] for _, logs in parts])
        heads.append(out.astype(jnp.bfloat16).T)
    rows = jnp.concatenate(heads, axis=1)
    y_parts, z_parts = out_ref.shape[:2]
    core = lax.axis_index("segment") % CORES
    for half, weight_ref in ((core, kept_ref), (1 - core, given_ref)):
        for y in range(y_parts // CORES):
            first = y * z_parts * HEAD_DIM
            block = weight_ref[:, :, first : first + z_parts * HEAD_DIM].reshape(-1, z_parts * HEAD_DIM)
            cols = jnp.dot(rows, block, preferred_element_type=jnp.float32).astype(jnp.bfloat16)
            for z in range(z_parts):
                out_ref[half * (y_parts // CORES) + y, z] = cols[:, z * HEAD_DIM : (z + 1) * HEAD_DIM]


def split_sum_body(parts_ref, own_ref, cross_ref):
    z = lax.axis_index("z")
    for ref, half in ((cross_ref, 1 - z), (own_ref, z)):
        ref[...] = functools.reduce(
            jnp.add, [parts_ref[i, half].astype(jnp.float32) for i in range(parts_ref.shape[0])]
        ).astype(jnp.bfloat16)


def shape(*dims):
    return jax.ShapeDtypeStruct(dims, jnp.bfloat16)


def on_device(queries, keys, values, lengths, selected, out_weight):
    rows = queries.shape[0]
    segments, z_parts, x_parts, y_parts = (lax.axis_size(a) for a in ("segment", "z", "x", "head"))
    message = x_parts * HEAD_DIM + STAT_ROWS
    tile = (rows, HEAD_DIM)

    def kernel(body, inputs, outputs, mib, **more):
        return pl.pallas_call(
            body,
            out_shape=outputs,
            in_specs=inputs,
            out_specs=whole(len(outputs)),
            compiler_params=pltpu.CompilerParams(vmem_limit_bytes=mib << 20),
            **more,
        )

    packed = out_weight.shape[1] // x_parts // CORES
    places = packed // HEAD_DIM
    vmem = pl.BlockSpec(memory_space=pltpu.VMEM)
    anywhere = pl.BlockSpec(memory_space=pl.ANY)
    own, cross = pl.pallas_call(
        attend_body,
        out_shape=[shape(message, rows)] * 2,
        in_specs=[pl.BlockSpec(memory_space=pltpu.SMEM)] * 2 + [anywhere] * 3,
        out_specs=[vmem] * 2,
        scratch_shapes=[
            pltpu.VMEM(queries.shape, jnp.bfloat16),
            pltpu.VMEM(keys.shape, jnp.bfloat16),
            pltpu.VMEM(values.shape, jnp.bfloat16),
            pltpu.VMEM((HEAD_DIM, keys.shape[0]), jnp.bfloat16),
            pltpu.SemaphoreType.DMA((3,)),
        ],
        name="attend",
    )(lengths, selected, queries, keys, values)
    pack = pl.pallas_call(
        pack_body,
        out_shape=shape(x_parts, HEAD_DIM, packed),
        in_specs=[anywhere],
        out_specs=anywhere,
        scratch_shapes=[
            pltpu.VMEM((x_parts, HEAD_DIM, packed), jnp.bfloat16),
            pltpu.SemaphoreType.DMA((x_parts, places)),
            pltpu.SemaphoreType.DMA((x_parts,)),
        ],
        name="pack",
    )(out_weight)

    def onward(part, flip):
        pairs = [
            (s * z_parts + z, (s + 1) % segments * z_parts + (z ^ flip))
            for s in range(segments)
            for z in range(z_parts)
        ]
        return lax.ppermute(part, ("segment", "z"), pairs)

    swap = [(s * z_parts + z, s * z_parts + 1 - z) for s in range(segments) for z in range(z_parts) if s % 2 or z == 0]
    other = lax.ppermute(cross, ("segment", "z"), swap)
    kept = lax.all_to_all(pack, "x", 0, 0, tiled=True)
    (terms,) = kernel(merge_body, whole(2), [shape(message, rows)], 8)(own, other)
    shared = [terms]
    for step in sorted(range(1, x_parts), key=lambda k: -min(k, x_parts - k)):
        shared.append(lax.ppermute(terms, "x", [(x, (x + step) % x_parts) for x in range(x_parts)]))
    given = lax.ppermute(kept, "segment", [(s, s ^ 1) for s in range(segments)])
    (products,) = kernel(project_body, whole(x_parts + 2), [shape(y_parts, z_parts, *tile)], 16)(*shared, kept, given)
    products = lax.all_to_all(products, "head", 0, 0, tiled=True)
    own, cross = kernel(split_sum_body, whole(1), [shape(*tile)] * 2, 8)(products)

    other = onward(cross, 1)
    own = onward(own, 0)
    return (own.astype(jnp.float32) + other.astype(jnp.float32)).astype(jnp.bfloat16)


def solution(mesh):
    segment, ctx, head = mesh.devices.shape
    split = jax.sharding.Mesh(
        mesh.devices.reshape(segment, Z_PARTS, ctx // Z_PARTS, head), ("segment", "z", "x", "head")
    )
    sections = ("segment", "z", "x")
    placed = (
        P("segment", "head"),
        P(sections, "head"),
        P(sections, "head"),
        P("segment"),
        P("segment", None),
        P(("head", "z", "x"), None),
    )
    return jax.shard_map(
        on_device,
        mesh=split,
        in_specs=placed,
        out_specs=P("segment", ("head", "z", "x")),
        check_vma=False,
    )
```
